512 devices in a mesh: pts: 64 (over y, x, core), tm: 8 (over z).
Axes of the slice: x: 4, y: 8, z: 8, core: 2. Of those that a mesh axis runs over, the one named last changes fastest.
Arguments:
- starting_location_factors: float32 [32768, 128], P('pts'), may hold values from -5 to 5
- starting_temporal_factors: float32 [8192, 128], P('tm'), may hold values from -5 to 5
- imposed_tension_record: float32 [32768, 8192], P('pts', 'tm'), may hold values from -10 to 10
- viscous_rate_factor: float32 [32768], P('pts'), may hold values from 0.2 to 1
- norton_power_law: float32 [32768], P('pts'), may hold values from 1.2 to 2.2
- space_inverse: float32 [128, 128], replicated, may hold values from -2 to 2
- time_inverse: float32 [128, 128], replicated, may hold values from -2 to 2
Outputs:
- space_out: float32 [32768, 128], P('pts')
- time_out: float32 [8192, 128], P('tm')
- misfit: float32 [2], replicated
The draws below stay inside these ranges and needn't reach their ends.
All inputs are finite; a program needn't handle non-finite values.
Results may differ from the reference program's by a relative error of at most 0.0005.
Values sent between devices are 32-bit elements; how exact they have to be, the bound alone decides.
A program may use at most 64 MiB of HBM per device.

```python
import math
import jax
import jax.numpy as jnp
from jax import lax

PRODUCT_TERMS = 128
ITERS = 2
LOCATIONS_IN_ROW = 512
LOCATION_AMOUNT = 32768
MOMENT_AMOUNT = 8192
N_PTS = 64


def near_identity(key):
    noise = jax.random.normal(key, (PRODUCT_TERMS, PRODUCT_TERMS), jnp.float32)
    return jnp.eye(PRODUCT_TERMS, dtype=jnp.float32) + 0.35 * noise / math.sqrt(PRODUCT_TERMS)


def draw_space_inverse(key, part):
    return near_identity(jax.random.fold_in(key, 11))


def draw_time_inverse(key, part):
    return near_identity(jax.random.fold_in(key, 23))


def draw_imposed_tension_record(key, part):
    inner = jax.random.fold_in(key, 37)
    shape = (LOCATION_AMOUNT, MOMENT_AMOUNT)
    ramp = jnp.arange(MOMENT_AMOUNT, dtype=jnp.float32) / max(MOMENT_AMOUNT - 1, 1)
    values = jax.random.truncated_normal(inner, -5.0, 5.0, shape, jnp.float32)
    amplitude = 0.5 + 1.5 * ramp
    return values * amplitude[None, :]


def block_levels(key, dims, cuts, smallest, top_value):
    loudness = 1.0
    for axis_at, shards_of in cuts:
        draws = jax.random.uniform(jax.random.fold_in(jax.random.fold_in(key, 6), axis_at), (shards_of,), jnp.float32, smallest / len(cuts), top_value / len(cuts))
        loudness = loudness * jnp.repeat(jnp.exp(draws), dims[axis_at] // shards_of).reshape((-1,) + (1,) * (len(dims) - 1 - axis_at))
    return loudness


def bell_draw(key, extent, width, limit, split=(), kind=jnp.bfloat16):
    drawn = jax.random.normal(key, extent, jnp.float32) * width
    if len(split) > 0:
        drawn = block_levels(key, extent, split, -0.22, 0.18) * drawn
    return jnp.clip(drawn, min=-limit, max=limit).astype(kind)


def setup_inputs(seed: int = 0) -> dict:
    key_of = jax.random.split(jax.random.key(seed), 8)
    starting_location_factors = bell_draw(key_of[0], (LOCATION_AMOUNT, PRODUCT_TERMS), 1.0, 5.0, ((0, 64),), jnp.float32)
    starting_temporal_factors = bell_draw(key_of[1], (MOMENT_AMOUNT, PRODUCT_TERMS), 1.0, 5.0, ((0, 8),), jnp.float32)
    imposed_tension_record = draw_imposed_tension_record(jax.random.fold_in(key_of[7], 71), 0)
    viscous_rate_factor = jnp.clip(jnp.exp(math.log(1.0) - 1.609438 * jax.random.uniform(key_of[3], (LOCATION_AMOUNT,), jnp.float32) ** block_levels(key_of[3], (LOCATION_AMOUNT,), ((0, 64),), -0.2, 0.2)), 0.2, 1.0)
    norton_power_law = jnp.clip(1.2 + 1.0 * jax.random.uniform(key_of[4], (LOCATION_AMOUNT,), jnp.float32) ** block_levels(key_of[4], (LOCATION_AMOUNT,), ((0, 64),), -0.2, 0.2), 1.2, 2.2)
    space_inverse = draw_space_inverse(jax.random.fold_in(key_of[7], 71), 0)
    time_inverse = draw_time_inverse(jax.random.fold_in(key_of[7], 71), 0)
    return dict(starting_location_factors=starting_location_factors, starting_temporal_factors=starting_temporal_factors, imposed_tension_record=imposed_tension_record, viscous_rate_factor=viscous_rate_factor, norton_power_law=norton_power_law, space_inverse=space_inverse, time_inverse=time_inverse)


highest = lax.Precision.HIGHEST

def viscous_pass(space_blk, starting_temporal_factors, load_blk, fluid_blk, expo_blk):
    rank_scale = 1.0 / math.sqrt(space_blk.shape[1])
    recon_field = jnp.dot(space_blk, starting_temporal_factors.T, precision=highest) * rank_scale
    stress = load_blk - recon_field
    flow_rate = fluid_blk[:, None] * stress * jnp.power(stress * stress + 1e-06, 0.5 * (expo_blk[:, None] - 1.0))
    return (stress, flow_rate)

def reference(starting_location_factors, starting_temporal_factors, imposed_tension_record, viscous_rate_factor, norton_power_law, space_inverse, time_inverse):
    residual_record = []
    for sweep in range(ITERS):
        location_groups = (imposed_tension_record.reshape(N_PTS, LOCATIONS_IN_ROW, MOMENT_AMOUNT), starting_location_factors.reshape(N_PTS, LOCATIONS_IN_ROW, PRODUCT_TERMS), viscous_rate_factor.reshape(N_PTS, LOCATIONS_IN_ROW), norton_power_law.reshape(N_PTS, LOCATIONS_IN_ROW))

        def one_block(running, inputs, starting_temporal_factors=starting_temporal_factors):
            time_acc, misfit_acc = running
            load_blk, space_blk, fluid_blk, expo_blk = inputs
            stress, flow_rate = viscous_pass(space_blk, starting_temporal_factors, load_blk, fluid_blk, expo_blk)
            time_acc = time_acc + lax.dot_general(flow_rate, space_blk, (((0,), (0,)), ((), ())), precision=highest)
            misfit_acc = misfit_acc + jnp.sum(stress * stress)
            return ((time_acc, misfit_acc), jnp.dot(flow_rate, starting_temporal_factors, precision=highest))
        starting_state = (jnp.zeros((MOMENT_AMOUNT, PRODUCT_TERMS), jnp.float32), jnp.zeros((), jnp.float32))
        (time_sum, residual_energy), space_blocks = lax.scan(one_block, starting_state, location_groups)
        space_sum = space_blocks.reshape(LOCATION_AMOUNT, PRODUCT_TERMS)
        temporal_factors_before_rescale = jnp.dot(time_sum, time_inverse, precision=highest)
        space_raw = jnp.dot(space_sum, space_inverse, precision=highest)
        space_sq = lax.optimization_barrier(jnp.sum(space_raw * space_raw, axis=0))
        temporal_magnitude_quad = lax.optimization_barrier(jnp.sum(temporal_factors_before_rescale * temporal_factors_before_rescale, axis=0))
        starting_location_factors = space_raw / jnp.sqrt(space_sq / LOCATION_AMOUNT + 1e-06)
        starting_temporal_factors = temporal_factors_before_rescale / jnp.sqrt(temporal_magnitude_quad / MOMENT_AMOUNT + 1e-06)
        residual_record.append(residual_energy / (LOCATION_AMOUNT * MOMENT_AMOUNT))
    return (starting_location_factors, starting_temporal_factors, jnp.stack(residual_record))
```

```python
import functools
import math

import jax
import jax.numpy as jnp
from jax import lax
from jax.experimental import pallas as pl
from jax.experimental.pallas import tpu as pltpu
from jax.sharding import PartitionSpec as P

ITERS = 2
F32, BF16 = jnp.float32, jnp.bfloat16
MESH = pl.DeviceIdType.MESH
NX, NY, NC = 4, 8, 2


def split(value):
    hi = value.astype(BF16)
    return hi, (value - hi.astype(F32)).astype(BF16)


def dot(a, b, ca, cb):
    return lax.dot_general(a, b, (((ca,), (cb,)), ((), ())), preferred_element_type=F32)


def fold(pair):
    return pair[:, :128] + pair[:, 128:]


def kernel(nz, s0, u0, sig, rate, power, inv_s, inv_t, s_out, u_out, mis_out,
           lr, ex, a_ref, b_ref, bb_ref, rec, fh, fl, tp, cr, th, xr, ts, yr, u_nx, sp, zr, s_nx, nv,
           send, recv):
    points, rank = s0.shape
    moments = u0.shape[0]
    half = moments // NC
    xrows = half // NX
    yrows = xrows // NY
    zrows = points // nz
    point_total = points * NX * NY * NC
    moment_total = moments * nz
    p, z = lax.axis_index("pts"), lax.axis_index("tm")
    c, x, y = p % NC, (p // NC) % NX, p // (NC * NX)

    def at(cc, xx, yy):
        return (yy * NX + xx) * NC + cc

    cx_peers = []
    for dc in range(NC):
        for dx in range(NX):
            if dc or dx:
                cx_peers.append(((c + dc) % NC, (x + dx) % NX))
    y_peers = [(y + d) % NY for d in range(1, NY)]
    z_peers = [(z + d) % nz for d in range(1, nz)]

    barrier = pltpu.get_barrier_semaphore()
    for cc, xx in cx_peers:
        pl.semaphore_signal(barrier, inc=1, device_id=(at(cc, xx, y), z), device_id_type=MESH)
    for yy in y_peers:
        pl.semaphore_signal(barrier, inc=1, device_id=(at(c, x, yy), z), device_id_type=MESH)
    for zz in z_peers:
        pl.semaphore_signal(barrier, inc=1, device_id=(p, zz), device_id_type=MESH)

    def put(src, dst, it, stage, pp, zz):
        pltpu.make_async_remote_copy(
            src_ref=src, dst_ref=dst, send_sem=send.at[it, stage], recv_sem=recv.at[it, stage],
            device_id=(pp, zz), device_id_type=MESH,
        ).start()

    def drain(ref, sem):
        pltpu.make_async_copy(ref, ref, sem).wait()

    for k in range(points // 128):
        rows = pl.ds(k * 128, 128)
        lr[rows, :] = jnp.broadcast_to(jnp.log2(rate[k : k + 1, :]), (128, 128)).T
        ex[rows, :] = jnp.broadcast_to(0.5 * (power[k : k + 1, :] - 1.0), (128, 128)).T

    scale_s = scale_u = None
    for it in range(ITERS):
        s_cur = s0 if it == 0 else s_nx.at[it - 1]
        u_cur = u0 if it == 0 else u_nx.at[it - 1]
        root = 1.0 / math.sqrt(rank)
        sv = s_cur[...] * (root if it == 0 else scale_s * scale_u * root)
        hi, lo = split(sv)
        a_ref[:, :128] = hi
        a_ref[:, 128:] = lo
        hi, lo = split(u_cur[...])
        b_ref[:, :128] = hi
        b_ref[:, 128:] = lo
        bb_ref[...] = hi

        def flow_block(j, mis):
            cols = pl.ds(pl.multiple_of(j * 256, 256), 256)
            ub = b_ref[cols, :]
            rec[...] = dot(a_ref[:, :128], ub[:, :128], 1, 1) + dot(a_ref[:, :128], ub[:, 128:], 1, 1) + dot(
                a_ref[:, 128:], ub[:, :128], 1, 1)
            for r in range(points // 64):
                rows = pl.ds(r * 64, 64)
                for h in range(2):
                    lanes = pl.ds(h * 128, 128)
                    cl = pl.ds(pl.multiple_of(j * 256 + h * 128, 128), 128)
                    stress = sig[rows, cl] - rec[rows, lanes]
                    quad = stress * stress
                    mis = mis + jnp.sum(quad.reshape(8, 8, 128), axis=0)
                    flow = stress * jnp.exp2(lr[rows, :] + ex[rows, :] * jnp.log2(quad + 1e-6))
                    hi, lo = split(flow)
                    fh[rows, cl] = hi
                    fl[rows, cl] = lo
            return mis

        mis = lax.fori_loop(0, moments // 256, flow_block, jnp.zeros((8, 128), F32))

        if it == 0:
            pl.semaphore_wait(barrier, len(cx_peers) + len(y_peers) + len(z_peers))

        def time_half(cc):
            cols = pl.ds(pl.multiple_of(cc * half, half), half)
            tp[it, cols, :] = fold(dot(fh[:, cols], a_ref[...], 0, 0) + dot(fl[:, cols], a_ref[...], 0, 0))
            return cols

        cols = time_half(1 - c)
        put(tp.at[it, cols, :], cr.at[it], it, 0, at(1 - c, x, y), z)
        cols = time_half(c)
        sp[it] = fold(dot(fh[...], b_ref[...], 1, 0) + dot(fl[...], b_ref[...], 1, 0))
        for d, zz in enumerate(z_peers):
            rows = pl.ds(pl.multiple_of(zz * zrows, zrows), zrows)
            put(sp.at[it, rows, :], zr.at[it, d], it, 1, p, zz)
        drain(cr.at[it], recv.at[it, 0])
        th[it] = tp[it, cols, :] + cr[it]
        for d in range(1, NX):
            xx = (x + d) % NX
            rows = pl.ds(pl.multiple_of(xx * xrows, xrows), xrows)
            put(th.at[it, rows, :], xr.at[it, d - 1], it, 2, at(c, xx, y), z)
        drain(xr.at[it], recv.at[it, 2])
        rows = pl.ds(pl.multiple_of(x * xrows, xrows), xrows)
        ts[it] = th[it, rows, :] + xr[it, 0] + xr[it, 1] + xr[it, 2]
        for d, yy in enumerate(y_peers):
            rows = pl.ds(pl.multiple_of(yy * yrows, yrows), yrows)
            put(ts.at[it, rows, :], yr.at[it, d], it, 3, at(c, x, yy), z)
        drain(zr.at[it], recv.at[it, 1])
        own_z = pl.ds(pl.multiple_of(z * zrows, zrows), zrows)
        piece = sp[it, own_z, :]
        for d in range(nz - 1):
            piece = piece + zr[it, d]
        if it > 0:
            piece = piece * scale_u
        s_raw = jnp.dot(piece, inv_s[...], precision=lax.Precision.HIGHEST, preferred_element_type=F32)
        s_nx[it, own_z, :] = s_raw
        for zz in z_peers:
            put(s_nx.at[it, own_z, :], s_nx.at[it, own_z, :], it, 4, p, zz)
        s_sq = jnp.sum(s_raw * s_raw, axis=0, keepdims=True)

        drain(yr.at[it], recv.at[it, 3])
        rows = pl.ds(pl.multiple_of(y * yrows, yrows), yrows)
        piece = ts[it, rows, :]
        for d in range(NY - 1):
            piece = piece + yr[it, d]
        piece = piece * (math.sqrt(rank) if it == 0 else math.sqrt(rank) / scale_u)
        t_raw = jnp.dot(piece, inv_t[...], precision=lax.Precision.HIGHEST, preferred_element_type=F32)
        own_t = pl.ds(pl.multiple_of(c * half + x * xrows + y * yrows, yrows), yrows)
        u_nx[it, own_t, :] = t_raw
        for yy in y_peers:
            put(u_nx.at[it, own_t, :], u_nx.at[it, own_t, :], it, 5, at(c, x, yy), z)
        t_sq = jnp.sum(t_raw * t_raw, axis=0, keepdims=True)

        mis = jnp.sum(mis, axis=0, keepdims=True)
        row = lax.broadcasted_iota(jnp.int32, (8, 128), 0)
        vec = jnp.where(row == 0, s_sq, jnp.where(row == 1, t_sq, jnp.where(row == 2, mis, 0.0)))
        me = c * NX + x
        nv[it, 0, me] = vec
        for cc, xx in cx_peers:
            put(nv.at[it, 0, me], nv.at[it, 0, me], it, 6, at(cc, xx, y), z)

        drain(yr.at[it], recv.at[it, 5])
        own_x = pl.ds(pl.multiple_of(c * half + x * xrows, xrows), xrows)
        for d in range(1, NX):
            put(u_nx.at[it, own_x, :], u_nx.at[it, own_x, :], it, 7, at(c, (x + d) % NX, y), z)

        drain(nv.at[it, 0, pl.ds(0, 7)], recv.at[it, 6])
        vec = nv[it, 0, 0]
        for k in range(1, 8):
            vec = vec + nv[it, 0, k]
        nv[it, 1, y] = vec
        for yy in y_peers:
            put(nv.at[it, 1, y], nv.at[it, 1, y], it, 8, at(c, x, yy), z)

        drain(xr.at[it], recv.at[it, 7])
        own_c = pl.ds(pl.multiple_of(c * half, half), half)
        put(u_nx.at[it, own_c, :], u_nx.at[it, own_c, :], it, 9, at(1 - c, x, y), z)

        drain(nv.at[it, 1, pl.ds(0, 7)], recv.at[it, 8])
        vec = nv[it, 1, 0]
        for k in range(1, 8):
            vec = vec + nv[it, 1, k]
        nv[it, 2, z] = vec
        for zz in z_peers:
            put(nv.at[it, 2, z], nv.at[it, 2, z], it, 10, p, zz)
        drain(cr.at[it], recv.at[it, 9])
        drain(zr.at[it], recv.at[it, 4])
        drain(nv.at[it, 2, pl.ds(0, 7)], recv.at[it, 10])
        vec = nv[it, 2, 0]
        for k in range(1, 8):
            vec = vec + nv[it, 2, k]
        scale_s = 1.0 / jnp.sqrt(vec[0:1, :] / point_total + 1e-6)
        scale_u = 1.0 / jnp.sqrt(vec[1:2, :] / moment_total + 1e-6)
        mis_out[it] = jnp.sum(vec[2:3, :]) / (point_total * moment_total)

    s_out[...] = s_nx[ITERS - 1] * scale_s
    u_out[...] = u_nx[ITERS - 1] * scale_u
    for it in range(ITERS):
        for stage, ref in enumerate((cr, zr, xr, yr, zr, yr, None, xr, None, cr, None)):
            drain(nv.at[it, 0, pl.ds(0, 7)] if ref is None else ref.at[it], send.at[it, stage])


def shards(nz, s0, u0, sig, rate, power, inv_s, inv_t):
    points, rank = s0.shape
    moments = u0.shape[0]
    half = moments // NC
    xrows = half // NX
    yrows = xrows // NY
    zrows = points // nz
    vmem = pl.BlockSpec(memory_space=pltpu.VMEM)
    return pl.pallas_call(
        functools.partial(kernel, nz),
        out_shape=(
            jax.ShapeDtypeStruct((points, rank), F32),
            jax.ShapeDtypeStruct((moments, rank), F32),
            jax.ShapeDtypeStruct((ITERS,), F32),
        ),
        in_specs=[vmem] * 7,
        out_specs=(vmem, vmem, pl.BlockSpec(memory_space=pltpu.SMEM)),
        scratch_shapes=[
            pltpu.VMEM((points, 128), F32),
            pltpu.VMEM((points, 128), F32),
            pltpu.VMEM((points, 2 * rank), BF16),
            pltpu.VMEM((moments, 2 * rank), BF16),
            pltpu.VMEM((moments, rank), BF16),
            pltpu.VMEM((points, 256), F32),
            pltpu.VMEM((points, moments), BF16),
            pltpu.VMEM((points, moments), BF16),
            pltpu.VMEM((ITERS, moments, rank), F32),
            pltpu.VMEM((ITERS, half, rank), F32),
            pltpu.VMEM((ITERS, half, rank), F32),
            pltpu.VMEM((ITERS, NX - 1, xrows, rank), F32),
            pltpu.VMEM((ITERS, xrows, rank), F32),
            pltpu.VMEM((ITERS, NY - 1, yrows, rank), F32),
            pltpu.VMEM((ITERS, moments, rank), F32),
            pltpu.VMEM((ITERS, points, rank), F32),
            pltpu.VMEM((ITERS, nz - 1, zrows, rank), F32),
            pltpu.VMEM((ITERS, points, rank), F32),
            pltpu.VMEM((ITERS, 3, 8, 8, 128), F32),
            pltpu.SemaphoreType.DMA((ITERS, 11)),
            pltpu.SemaphoreType.DMA((ITERS, 11)),
        ],
        compiler_params=pltpu.CompilerParams(
            collective_id=0, has_side_effects=True, vmem_limit_bytes=40 * 1024 * 1024
        ),
    )(s0, u0, sig, rate.reshape(points // 128, 128), power.reshape(points // 128, 128), inv_s, inv_t)


def solution(mesh):
    return jax.shard_map(
        functools.partial(shards, mesh.shape["tm"]),
        mesh=mesh,
        in_specs=(P("pts", None), P("tm", None), P("pts", "tm"), P("pts"), P("pts"), P(), P()),
        out_specs=(P("pts", None), P("tm", None), P()),
        check_vma=False,
    )
```

```python
import functools
import math

import jax
import jax.numpy as jnp
from jax import lax
from jax.experimental import pallas as pl
from jax.experimental.pallas import tpu as pltpu
from jax.sharding import PartitionSpec as P

ITERS = 2
F32, BF16 = jnp.float32, jnp.bfloat16
MESH = pl.DeviceIdType.MESH
NX, NY, NC = 4, 8, 2
ORDER = (2, 1, 3, 0)
X_SUM, Y_SUM, Z_SUM, Z_ALL, Y_ALL, X_ALL, C_ALL, N_CX, N_Y, N_Z, STAGES = range(2, 13)


def split(value):
    hi = value.astype(BF16)
    return hi, (value - hi.astype(F32)).astype(BF16)


def dot(a, b, ca, cb):
    return lax.dot_general(a, b, (((ca,), (cb,)), ((), ())), preferred_element_type=F32)


def kernel(nz, s_in, u_in, sig_in, rate_in, power_in, inv_s_in, inv_t_in, s_out, u_out, mis_out,
           s0, u0, sig, rate, power, inv_s, inv_t,
           lr, ex, a_ref, at_ref, b_ref, rec, fh, fl, tp, cr, th, xr, ts, yr, u_nx, sp, zr, s_nx, nv,
           load, send, recv):
    points, rank = s0.shape
    moments = u0.shape[0]
    half = moments // NC
    xrows = half // NX
    yrows = xrows // NY
    zrows = points // nz
    blocks = moments // xrows
    point_total = points * NX * NY * NC
    moment_total = moments * nz
    p, z = lax.axis_index("pts"), lax.axis_index("tm")
    c, x, y = p % NC, (p // NC) % NX, p // (NC * NX)

    def at(cc, xx, yy):
        return (yy * NX + xx) * NC + cc

    cx_peers = []
    for dc in range(NC):
        for dx in range(NX):
            if dc or dx:
                cx_peers.append(((c + dc) % NC, (x + dx) % NX))
    y_peers = [(y + d) % NY for d in range(1, NY)]
    z_peers = [(z + d) % nz for d in range(1, nz)]

    starts = []
    for side in (1 - c, c):
        for d in ORDER:
            starts.append(pl.multiple_of(side * half + (x + d) % NX * xrows, xrows))

    loads = []

    def fetch(src, dst):
        cp = pltpu.make_async_copy(src, dst, load.at[len(loads)])
        cp.start()
        loads.append(cp)
        return cp

    u_load, s_load = fetch(u_in, u0), fetch(s_in, s0)
    rate_load, power_load = fetch(rate_in, rate), fetch(power_in, power)
    sig_load = [fetch(sig_in.at[:, pl.ds(q, xrows)], sig.at[k]) for k, q in enumerate(starts)]
    inv_loads = [fetch(inv_s_in, inv_s), fetch(inv_t_in, inv_t)]

    barrier = pltpu.get_barrier_semaphore()
    for cc, xx in cx_peers:
        pl.semaphore_signal(barrier, inc=1, device_id=(at(cc, xx, y), z), device_id_type=MESH)
    for yy in y_peers:
        pl.semaphore_signal(barrier, inc=1, device_id=(at(c, x, yy), z), device_id_type=MESH)
    for zz in z_peers:
        pl.semaphore_signal(barrier, inc=1, device_id=(p, zz), device_id_type=MESH)

    def put(src, dst, it, stage, pp, zz):
        pltpu.make_async_remote_copy(
            src_ref=src, dst_ref=dst, send_sem=send.at[it, stage], recv_sem=recv.at[it, stage],
            device_id=(pp, zz), device_id_type=MESH,
        ).start()

    def drain(ref, sem, it, stage):
        pltpu.make_async_copy(ref, ref, sem.at[it, stage]).wait()

    def split_time(u_cur):
        for k, q in enumerate(starts):
            rows = pl.ds(k * xrows, xrows)
            hi, lo = split(u_cur[pl.ds(q, xrows), :])
            b_ref[rows, :rank] = hi
            b_ref[rows, rank : 2 * rank] = hi
            b_ref[rows, 2 * rank : 3 * rank] = lo
            b_ref[rows, 3 * rank :] = lo

    rate_load.wait()
    power_load.wait()
    for k in range(points // 128):
        rows = pl.ds(k * 128, 128)
        lr[rows, :] = jnp.broadcast_to(jnp.log2(rate[k : k + 1, :]), (128, 128)).T
        ex[rows, :] = jnp.broadcast_to(0.5 * (power[k : k + 1, :] - 1.0), (128, 128)).T
    u_load.wait()
    split_time(u0)
    s_load.wait()

    scale_s = scale_u = None
    for it in range(ITERS):
        s_cur = s0 if it == 0 else s_nx.at[it - 1]
        root = 1.0 / math.sqrt(rank)
        factor = root if it == 0 else scale_s * scale_u * root
        for k in range(points // 128):
            rows = pl.ds(k * 128, 128)
            sv = s_cur[rows, :] * factor
            hi, lo = split(sv)
            a_ref[rows, :rank] = hi
            a_ref[rows, rank:] = lo
            hi, lo = split(sv.T)
            at_ref[:rank, rows] = hi
            at_ref[rank:, rows] = lo

        def rebuild(m):
            rows = pl.ds(2 * m * xrows, 2 * xrows)
            rec[m % 2] = dot(a_ref[...], b_ref[rows, : 2 * rank], 1, 1) + dot(a_ref[...], b_ref[rows, 2 * rank :], 1, 1)

        def respond(m, mis):
            for k in (2 * m, 2 * m + 1):
                lanes = pl.ds(k * xrows, xrows)
                for r in range(points // 64):
                    rows = pl.ds(r * 64, 64)
                    stress = sig[k, rows, :] - rec[m % 2, rows, pl.ds((k % 2) * xrows, xrows)]
                    quad = stress * stress
                    mis = mis + jnp.sum(quad.reshape(8, 8, 128), axis=0)
                    flow = stress * jnp.exp2(lr[rows, :] + ex[rows, :] * jnp.log2(quad + 1e-6))
                    hi, lo = split(flow)
                    fh[rows, lanes] = hi
                    fl[rows, lanes] = lo
            return mis

        def time_part(m):
            lanes = pl.ds(2 * m * xrows, 2 * xrows)
            pair = dot(at_ref[...], fh[:, lanes], 1, 0)
            part = pair[:rank] + pair[rank:] + dot(at_ref[:rank, :], fl[:, lanes], 1, 0)
            return part[:, :xrows].T, part[:, xrows:].T

        def space_part(m):
            lanes = pl.ds(m * half, half)
            pair = dot(fh[:, lanes], b_ref[lanes, rank : 3 * rank], 1, 0)
            return pair[:, :rank] + pair[:, rank:] + dot(fl[:, lanes], b_ref[lanes, :rank], 1, 0)

        def send_core(m, parts):
            for j in range(2):
                tp[it, 2 * m + j] = parts[j]
            two = pl.ds(2 * m, 2)
            put(tp.at[it, two], cr.at[it, two], it, m, at(1 - c, x, y), z)

        def send_x(m, parts):
            drain(cr.at[it, pl.ds(2 * m, 2)], recv, it, m)
            for j in (2 * m, 2 * m + 1):
                th[it, j] = parts[j % 2] + cr[it, j]
                d = ORDER[j]
                if d:
                    put(th.at[it, j], xr.at[it, d - 1], it, X_SUM, at(c, (x + d) % NX, y), z)

        def arrive(m):
            if it == 0:
                sig_load[2 * m].wait()
                sig_load[2 * m + 1].wait()

        mis = jnp.zeros((8, 128), F32)
        rebuild(0)
        arrive(0)
        rebuild(1)
        mis = respond(0, mis)
        arrive(1)
        rebuild(2)
        mis = respond(1, mis)
        parts = time_part(0)
        if it == 0:
            pl.semaphore_wait(barrier, len(cx_peers) + len(y_peers) + len(z_peers))
        send_core(0, parts)
        arrive(2)
        rebuild(3)
        mis = respond(2, mis)
        send_core(1, time_part(1))
        arrive(3)
        mis = respond(3, mis)
        parts = time_part(2)
        sp[it] = space_part(0)
        send_x(0, parts)
        send_x(1, time_part(3))
        sp[it] = sp[it] + space_part(1)
        for d, zz in enumerate(z_peers):
            rows = pl.ds(pl.multiple_of(zz * zrows, zrows), zrows)
            put(sp.at[it, rows, :], zr.at[it, d], it, Z_SUM, p, zz)
        drain(xr.at[it], recv, it, X_SUM)
        ts[it] = th[it, NX - 1] + xr[it, 0] + xr[it, 1] + xr[it, 2]
        for d, yy in enumerate(y_peers):
            rows = pl.ds(pl.multiple_of(yy * yrows, yrows), yrows)
            put(ts.at[it, rows, :], yr.at[it, d], it, Y_SUM, at(c, x, yy), z)
        if it == 0:
            for cp in inv_loads:
                cp.wait()
        drain(zr.at[it], recv, it, Z_SUM)
        own_z = pl.ds(pl.multiple_of(z * zrows, zrows), zrows)
        piece = sp[it, own_z, :]
        for d in range(nz - 1):
            piece = piece + zr[it, d]
        if it > 0:
            piece = piece * scale_u
        s_raw = jnp.dot(piece, inv_s[...], precision=lax.Precision.HIGHEST, preferred_element_type=F32)
        s_nx[it, own_z, :] = s_raw
        for zz in z_peers:
            put(s_nx.at[it, own_z, :], s_nx.at[it, own_z, :], it, Z_ALL, p, zz)
        s_sq = jnp.sum(s_raw * s_raw, axis=0, keepdims=True)

        drain(yr.at[it], recv, it, Y_SUM)
        rows = pl.ds(pl.multiple_of(y * yrows, yrows), yrows)
        piece = ts[it, rows, :]
        for d in range(NY - 1):
            piece = piece + yr[it, d]
        piece = piece * (math.sqrt(rank) if it == 0 else math.sqrt(rank) / scale_u)
        t_raw = jnp.dot(piece, inv_t[...], precision=lax.Precision.HIGHEST, preferred_element_type=F32)
        own_t = pl.ds(pl.multiple_of(c * half + x * xrows + y * yrows, yrows), yrows)
        u_nx[it, own_t, :] = t_raw
        t_sq = jnp.sum(t_raw * t_raw, axis=0, keepdims=True)

        mis = jnp.sum(mis, axis=0, keepdims=True)
        row = lax.broadcasted_iota(jnp.int32, (8, 128), 0)
        vec = jnp.where(row == 0, s_sq, jnp.where(row == 1, t_sq, jnp.where(row == 2, mis, 0.0)))
        me = c * NX + x
        nv[it, 0, me] = vec
        for cc, xx in cx_peers:
            put(nv.at[it, 0, me], nv.at[it, 0, me], it, N_CX, at(cc, xx, y), z)
        for yy in y_peers:
            put(u_nx.at[it, own_t, :], u_nx.at[it, own_t, :], it, Y_ALL, at(c, x, yy), z)

        drain(nv.at[it, 0, pl.ds(0, 7)], recv, it, N_CX)
        vec = nv[it, 0, 0]
        for k in range(1, NC * NX):
            vec = vec + nv[it, 0, k]
        nv[it, 1, y] = vec
        for yy in y_peers:
            put(nv.at[it, 1, y], nv.at[it, 1, y], it, N_Y, at(c, x, yy), z)

        drain(yr.at[it], recv, it, Y_ALL)
        own_x = pl.ds(pl.multiple_of(c * half + x * xrows, xrows), xrows)
        for d in ORDER[: NX - 1]:
            put(u_nx.at[it, own_x, :], u_nx.at[it, own_x, :], it, X_ALL, at(c, (x + d) % NX, y), z)

        drain(nv.at[it, 1, pl.ds(0, 7)], recv, it, N_Y)
        vec = nv[it, 1, 0]
        for k in range(1, NY):
            vec = vec + nv[it, 1, k]
        nv[it, 2, z] = vec
        for zz in z_peers:
            put(nv.at[it, 2, z], nv.at[it, 2, z], it, N_Z, p, zz)

        drain(xr.at[it], recv, it, X_ALL)
        own_c = pl.ds(pl.multiple_of(c * half, half), half)
        put(u_nx.at[it, own_c, :], u_nx.at[it, own_c, :], it, C_ALL, at(1 - c, x, y), z)
        drain(cr.at[it], recv, it, C_ALL)
        if it + 1 < ITERS:
            split_time(u_nx.at[it])
        drain(zr.at[it], recv, it, Z_ALL)
        drain(nv.at[it, 2, pl.ds(0, 7)], recv, it, N_Z)
        vec = nv[it, 2, 0]
        for k in range(1, nz):
            vec = vec + nv[it, 2, k]
        scale_s = 1.0 / jnp.sqrt(vec[0:1, :] / point_total + 1e-6)
        scale_u = 1.0 / jnp.sqrt(vec[1:2, :] / moment_total + 1e-6)
        mis_out[it : it + 1, :] = vec[2:3, :] / (point_total * moment_total)

    s_out[...] = s_nx[ITERS - 1] * scale_s
    u_out[...] = u_nx[ITERS - 1] * scale_u
    for it in range(ITERS):
        for m in range(2):
            drain(cr.at[it, pl.ds(2 * m, 2)], send, it, m)
        small = nv.at[it, 0, pl.ds(0, 7)]
        for stage, ref in (
            (X_SUM, xr.at[it]), (Y_SUM, yr.at[it]), (Z_SUM, zr.at[it]), (Z_ALL, zr.at[it]), (Y_ALL, yr.at[it]),
            (X_ALL, xr.at[it]), (C_ALL, cr.at[it]), (N_CX, small), (N_Y, small), (N_Z, small),
        ):
            drain(ref, send, it, stage)


def store(s, u, mis, s_out, u_out, mis_out, sem):
    copies = [pltpu.make_async_copy(u, u_out, sem.at[0]), pltpu.make_async_copy(s, s_out, sem.at[1])]
    for cp in copies:
        cp.start()
    for k in range(ITERS):
        mis_out[k] = jnp.sum(mis[k : k + 1, :])
    for cp in copies:
        cp.wait()


def shards(nz, s0, u0, sig, rate, power, inv_s, inv_t):
    points, rank = s0.shape
    moments = u0.shape[0]
    half = moments // NC
    xrows = half // NX
    yrows = xrows // NY
    zrows = points // nz
    blocks = moments // xrows
    vmem, smem = pl.BlockSpec(memory_space=pltpu.VMEM), pl.BlockSpec(memory_space=pltpu.SMEM)
    hbm = pl.BlockSpec(memory_space=pltpu.HBM)
    outs = (
        jax.ShapeDtypeStruct((points, rank), F32),
        jax.ShapeDtypeStruct((moments, rank), F32),
        jax.ShapeDtypeStruct((ITERS,), F32),
    )
    modes = pl.pallas_call(
        functools.partial(kernel, nz),
        out_shape=outs[:2] + (jax.ShapeDtypeStruct((ITERS, 128), F32),),
        in_specs=[hbm] * 7,
        out_specs=(vmem, vmem, vmem),
        scratch_shapes=[
            pltpu.VMEM((points, rank), F32),
            pltpu.VMEM((moments, rank), F32),
            pltpu.VMEM((blocks, points, xrows), F32),
            pltpu.VMEM((points // 128, 128), F32),
            pltpu.VMEM((points // 128, 128), F32),
            pltpu.VMEM((rank, rank), F32),
            pltpu.VMEM((rank, rank), F32),
            pltpu.VMEM((points, 128), F32),
            pltpu.VMEM((points, 128), F32),
            pltpu.VMEM((points, 2 * rank), BF16),
            pltpu.VMEM((2 * rank, points), BF16),
            pltpu.VMEM((moments, 4 * rank), BF16),
            pltpu.VMEM((2, points, 2 * xrows), F32),
            pltpu.VMEM((points, moments), BF16),
            pltpu.VMEM((points, moments), BF16),
            pltpu.VMEM((ITERS, NX, xrows, rank), F32),
            pltpu.VMEM((ITERS, NX, xrows, rank), F32),
            pltpu.VMEM((ITERS, NX, xrows, rank), F32),
            pltpu.VMEM((ITERS, NX - 1, xrows, rank), F32),
            pltpu.VMEM((ITERS, xrows, rank), F32),
            pltpu.VMEM((ITERS, NY - 1, yrows, rank), F32),
            pltpu.VMEM((ITERS, moments, rank), F32),
            pltpu.VMEM((ITERS, points, rank), F32),
            pltpu.VMEM((ITERS, nz - 1, zrows, rank), F32),
            pltpu.VMEM((ITERS, points, rank), F32),
            pltpu.VMEM((ITERS, 3, 8, 8, 128), F32),
            pltpu.SemaphoreType.DMA((6 + blocks,)),
            pltpu.SemaphoreType.DMA((ITERS, STAGES)),
            pltpu.SemaphoreType.DMA((ITERS, STAGES)),
        ],
        compiler_params=pltpu.CompilerParams(
            collective_id=0, has_side_effects=True, vmem_limit_bytes=40 * 1024 * 1024
        ),
    )(*[pltpu.with_memory_space_constraint(v, pltpu.HBM) for v in (
        s0, u0, sig, rate.reshape(points // 128, 128), power.reshape(points // 128, 128), inv_s, inv_t)])
    return pl.pallas_call(
        store,
        out_shape=outs,
        in_specs=[vmem, vmem, vmem],
        out_specs=(hbm, hbm, smem),
        scratch_shapes=[pltpu.SemaphoreType.DMA((2,))],
    )(*[pltpu.with_memory_space_constraint(v, pltpu.VMEM) for v in modes])


def solution(mesh):
    return jax.shard_map(
        functools.partial(shards, mesh.shape["tm"]),
        mesh=mesh,
        in_specs=(P("pts", None), P("tm", None), P("pts", "tm"), P("pts"), P("pts"), P(), P()),
        out_specs=(P("pts", None), P("tm", None), P()),
        check_vma=False,
    )
```

```python
import functools
import math

import jax
import jax.numpy as jnp
from jax import lax
from jax.experimental import pallas as pl
from jax.experimental.pallas import tpu as pltpu
from jax.sharding import PartitionSpec as P

ITERS = 2
F32, BF16 = jnp.float32, jnp.bfloat16
MESH = pl.DeviceIdType.MESH
NX, NY, NC = 4, 8, 2
ORDER = (2, 1, 3, 0)
NEAR = (1, 7, 2, 6, 3, 5, 4)
X_SUM, Y_SUM, Z_SUM, Z_ALL, C_ALL, N_XY, N_Z, M_CX, M_Y, M_Z, Y_ALL = range(2, 13)
X_ALL = Y_ALL + NY
STAGES = X_ALL + NY


def split(value):
    hi = value.astype(BF16)
    return hi, (value - hi.astype(F32)).astype(BF16)


def dot(a, b, ca, cb):
    return lax.dot_general(a, b, (((ca,), (cb,)), ((), ())), preferred_element_type=F32)


def kernel(nz, s_in, u_in, sig_in, rate_in, power_in, inv_s_in, inv_t_in, s_out, u_out, mis_out,
           s0, u0, sig, rate, power, inv_s, inv_t,
           sig_lr, sig_ex, lr, ex, a_ref, at_ref, b_ref, rec, fh, fl, tp, cr, th, xr, ts, yr, u_nx, sp, zr, s_nx, nv, n_xy, n_z,
           load, send, recv):
    points, rank = s0.shape
    moments = u0.shape[0]
    half = moments // NC
    xrows = half // NX
    yrows = xrows // NY
    zrows = points // nz
    blocks = moments // xrows
    point_total = points * NX * NY * NC
    moment_total = moments * nz
    p, z = lax.axis_index("pts"), lax.axis_index("tm")
    c, x, y = p % NC, (p // NC) % NX, p // (NC * NX)

    def at(cc, xx, yy):
        return (yy * NX + xx) * NC + cc

    cx_peers = []
    for dc in range(NC):
        for dx in range(NX):
            if dc or dx:
                cx_peers.append(((c + dc) % NC, (x + dx) % NX))
    y_peers = [(y + d) % NY for d in NEAR[::-1]]
    z_far = sorted(range(1, nz), key=lambda d: -min(d, nz - d))
    z_peers = [(z + d) % nz for d in z_far]
    turned = [pl.multiple_of(zz * zrows, zrows) for zz in z_peers + [z]]
    plane = []
    for dy in NEAR[::-1] + (0,):
        for dx in ORDER:
            for dc in (1, 0):
                if dc or dx or dy:
                    plane.append(at((c + dc) % NC, (x + dx) % NX, (y + dy) % NY))

    starts = []
    for side in (1 - c, c):
        for d in ORDER:
            starts.append(pl.multiple_of(side * half + (x + d) % NX * xrows, xrows))

    loads = []

    def fetch(src, dst):
        cp = pltpu.make_async_copy(src, dst, load.at[len(loads)])
        cp.start()
        loads.append(cp)
        return cp

    u_load, s_load = fetch(u_in, u0), fetch(s_in, s0)
    rate_load, power_load = fetch(rate_in, rate), fetch(power_in, power)
    sig_load = [fetch(sig_in.at[:, pl.ds(q, xrows)], sig.at[k]) for k, q in enumerate(starts)]
    inv_loads = [fetch(inv_s_in, inv_s), fetch(inv_t_in, inv_t)]

    barrier = pltpu.get_barrier_semaphore()
    for pp in plane:
        pl.semaphore_signal(barrier, inc=1, device_id=(pp, z), device_id_type=MESH)
    for zz in z_peers:
        pl.semaphore_signal(barrier, inc=1, device_id=(p, zz), device_id_type=MESH)

    def put(src, dst, it, stage, pp, zz):
        pltpu.make_async_remote_copy(
            src_ref=src, dst_ref=dst, send_sem=send.at[it, stage], recv_sem=recv.at[it, stage],
            device_id=(pp, zz), device_id_type=MESH,
        ).start()

    def drain(ref, sem, it, stage):
        pltpu.make_async_copy(ref, ref, sem.at[it, stage]).wait()

    def split_time(u_cur, slots):
        for k in slots:
            q = starts[k]
            rows = pl.ds(k * xrows, xrows)
            hi, lo = split(u_cur[pl.ds(q, xrows), :])
            b_ref[rows, :rank] = hi
            b_ref[rows, rank : 2 * rank] = hi
            b_ref[rows, 2 * rank : 3 * rank] = lo
            b_ref[rows, 3 * rank :] = lo

    def total(ref, count):
        sums = [ref[k] for k in range(4)]
        for k in range(4, count):
            sums[k % 4] = sums[k % 4] + ref[k]
        return (sums[0] + sums[1]) + (sums[2] + sums[3])

    rate_load.wait()
    power_load.wait()
    for k in range(points // 128):
        rows = pl.ds(k * 128, 128)
        sig_lr[rows, :] = jnp.broadcast_to(jnp.log2(rate[k : k + 1, :]), (128, 128)).T
        sig_ex[rows, :] = jnp.broadcast_to(0.5 * (power[k : k + 1, :] - 1.0), (128, 128)).T
    for r, q in enumerate(turned):
        rows = pl.ds(r * zrows, zrows)
        lr[rows, :] = sig_lr[pl.ds(q, zrows), :]
        ex[rows, :] = sig_ex[pl.ds(q, zrows), :]
    u_load.wait()
    split_time(u0, range(blocks))
    s_load.wait()

    scale_s = scale_u = None
    for it in range(ITERS):
        s_cur = s0 if it == 0 else s_nx.at[it - 1]
        root = 1.0 / math.sqrt(rank)
        factor = root if it == 0 else scale_s * scale_u * root
        for k in range(nz // 2):
            rows = pl.ds(2 * k * zrows, 2 * zrows)
            sv = jnp.concatenate([s_cur[pl.ds(q, zrows), :] for q in turned[2 * k : 2 * k + 2]], axis=0) * factor
            hi, lo = split(sv)
            a_ref[rows, :rank] = hi
            a_ref[rows, rank:] = lo
            hi, lo = split(sv.T)
            at_ref[:rank, rows] = hi
            at_ref[rank:, rows] = lo

        def rebuild(m):
            rows = pl.ds(2 * m * xrows, 2 * xrows)
            for pts in (pl.ds(0, points // 2), pl.ds(points // 2, points // 2)):
                rec[m % 2, pts, :] = dot(a_ref[pts, :], b_ref[rows, : 2 * rank], 1, 1) + dot(
                    a_ref[pts, :], b_ref[rows, 2 * rank :], 1, 1)

        def respond(m, mis):
            for k in (2 * m, 2 * m + 1):
                lanes = pl.ds(k * xrows, xrows)
                for r, q in enumerate(turned):
                    rows = pl.ds(r * zrows, zrows)
                    stress = sig[k, pl.ds(q, zrows), :] - rec[m % 2, rows, pl.ds((k % 2) * xrows, xrows)]
                    quad = stress * stress
                    mis = mis + jnp.sum(quad.reshape(zrows // 8, 8, 128), axis=0)
                    flow = stress * jnp.exp2(lr[rows, :] + ex[rows, :] * jnp.log2(quad + 1e-6))
                    hi, lo = split(flow)
                    fh[rows, lanes] = hi
                    fl[rows, lanes] = lo
            return mis

        def time_part(m):
            lanes = pl.ds(2 * m * xrows, 2 * xrows)
            pair = dot(at_ref[...], fh[:, lanes], 1, 0)
            part = pair[:rank] + pair[rank:] + dot(at_ref[:rank, :], fl[:, lanes], 1, 0)
            return part[:, :xrows].T, part[:, xrows:].T

        def send_space(h):
            pts = pl.ds(h * (points // 2), points // 2)
            pair = dot(fh[pts, :], b_ref[:, rank : 3 * rank], 1, 0)
            sp[it, pts, :] = pair[:, :rank] + pair[:, rank:] + dot(fl[pts, :], b_ref[:, :rank], 1, 0)
            for r in range(h * nz // 2, min((h + 1) * nz // 2, nz - 1)):
                put(sp.at[it, pl.ds(r * zrows, zrows), :], zr.at[it, r], it, Z_SUM, p, z_peers[r])

        def send_core(m, parts):
            for j in range(2):
                tp[it, 2 * m + j] = parts[j]
            two = pl.ds(2 * m, 2)
            put(tp.at[it, two], cr.at[it, two], it, m, at(1 - c, x, y), z)

        def send_x(m, parts):
            drain(cr.at[it, pl.ds(2 * m, 2)], recv, it, m)
            for j in (2 * m, 2 * m + 1):
                th[it, j] = parts[j % 2] + cr[it, j]
                d = ORDER[j]
                if d:
                    put(th.at[it, j], xr.at[it, d - 1], it, X_SUM, at(c, (x + d) % NX, y), z)

        def arrive(m):
            if it == 0:
                sig_load[2 * m].wait()
                sig_load[2 * m + 1].wait()

        mis = jnp.zeros((8, 128), F32)
        rebuild(0)
        arrive(0)
        rebuild(1)
        mis = respond(0, mis)
        parts = time_part(0)
        if it == 0:
            pl.semaphore_wait(barrier, len(plane) + len(z_peers))
        send_core(0, parts)
        arrive(1)
        rebuild(2)
        mis = respond(1, mis)
        send_core(1, time_part(1))
        arrive(2)
        rebuild(3)
        mis = respond(2, mis)
        send_x(0, time_part(2))
        arrive(3)
        mis = respond(3, mis)
        send_x(1, time_part(3))
        send_space(0)
        send_space(1)
        me = c * NX + x
        nv[it, 0, me] = jnp.sum(mis, axis=0, keepdims=True)
        for cc, xx in cx_peers:
            put(nv.at[it, 0, me], nv.at[it, 0, me], it, M_CX, at(cc, xx, y), z)

        drain(xr.at[it], recv, it, X_SUM)
        ts[it] = th[it, NX - 1] + xr[it, 0] + xr[it, 1] + xr[it, 2]
        for d, yy in enumerate(y_peers):
            rows = pl.ds(pl.multiple_of(yy * yrows, yrows), yrows)
            put(ts.at[it, rows, :], yr.at[it, d], it, Y_SUM, at(c, x, yy), z)
        if it == 0:
            for cp in inv_loads:
                cp.wait()
        drain(nv.at[it, 0, pl.ds(0, 7)], recv, it, M_CX)
        nv[it, 1, y] = total(nv.at[it, 0], NC * NX)
        for yy in y_peers:
            put(nv.at[it, 1, y], nv.at[it, 1, y], it, M_Y, at(c, x, yy), z)

        def piece_rows(xx, yy):
            return pl.ds(pl.multiple_of(c * half + xx * xrows + yy * yrows, yrows), yrows)

        def pass_x(dy):
            rows = piece_rows(x, (y + NY - dy) % NY)
            for d in ORDER[: NX - 1]:
                put(u_nx.at[it, rows, :], u_nx.at[it, rows, :], it, X_ALL + dy, at(c, (x + d) % NX, y), z)

        def pass_core(dy):
            drain(xr.at[it, 0, pl.ds(0, (NX - 1) * yrows)], recv, it, X_ALL + dy)
            for d in ORDER[: NX - 1]:
                rows = piece_rows((x + d) % NX, (y + NY - dy) % NY)
                put(u_nx.at[it, rows, :], u_nx.at[it, rows, :], it, C_ALL, at(1 - c, x, y), z)

        drain(zr.at[it], recv, it, Z_SUM)
        own_z = pl.ds(pl.multiple_of(z * zrows, zrows), zrows)
        piece = sp[it, pl.ds((nz - 1) * zrows, zrows), :]
        for d in range(nz - 1):
            piece = piece + zr[it, d]
        if it > 0:
            piece = piece * scale_u
        s_raw = jnp.dot(piece, inv_s[...], precision=lax.Precision.HIGHEST, preferred_element_type=F32)
        s_nx[it, own_z, :] = s_raw
        n_xy[it, p, :, :rank] = jnp.sum(s_raw * s_raw, axis=0, keepdims=True)
        for zz in z_peers:
            put(s_nx.at[it, own_z, :], s_nx.at[it, own_z, :], it, Z_ALL, p, zz)

        drain(yr.at[it], recv, it, Y_SUM)
        rows = pl.ds(pl.multiple_of(y * yrows, yrows), yrows)
        piece = ts[it, rows, :]
        for d in range(NY - 1):
            piece = piece + yr[it, d]
        piece = piece * (math.sqrt(rank) if it == 0 else math.sqrt(rank) / scale_u)
        t_raw = jnp.dot(piece, inv_t[...], precision=lax.Precision.HIGHEST, preferred_element_type=F32)
        own_t = piece_rows(x, y)
        u_nx[it, own_t, :] = t_raw
        n_xy[it, p, :, rank:] = jnp.sum(t_raw * t_raw, axis=0, keepdims=True)
        for pp in plane:
            put(n_xy.at[it, p], n_xy.at[it, p], it, N_XY, pp, z)
        for d in NEAR[::-1]:
            put(u_nx.at[it, own_t, :], u_nx.at[it, own_t, :], it, Y_ALL + d, at(c, x, (y + d) % NY), z)
        pass_x(0)

        drain(nv.at[it, 1, pl.ds(0, 7)], recv, it, M_Y)
        nv[it, 2, z] = total(nv.at[it, 1], NY)
        for zz in z_peers:
            put(nv.at[it, 2, z], nv.at[it, 2, z], it, M_Z, p, zz)

        for d in NEAR:
            drain(u_nx.at[it, piece_rows(x, (y + NY - d) % NY), :], recv, it, Y_ALL + d)
            pass_x(d)
        drain(n_xy.at[it, pl.ds(0, len(plane))], recv, it, N_XY)
        n_z[it, z] = total(n_xy.at[it], len(plane) + 1)
        for zz in z_peers:
            put(n_z.at[it, z], n_z.at[it, z], it, N_Z, p, zz)
        own = pl.ds(pl.multiple_of(c * half + x * xrows, xrows), xrows)
        put(u_nx.at[it, own, :], u_nx.at[it, own, :], it, C_ALL, at(1 - c, x, y), z)
        for d in (0,) + NEAR[:2]:
            pass_core(d)
        for d in NEAR[2:]:
            pass_core(d)
        if it + 1 < ITERS:
            split_time(u_nx.at[it], range(NX, 2 * NX))
        drain(cr.at[it], recv, it, C_ALL)
        if it + 1 < ITERS:
            split_time(u_nx.at[it], range(NX))
        drain(zr.at[it], recv, it, Z_ALL)
        drain(nv.at[it, 2, pl.ds(0, 7)], recv, it, M_Z)
        mis_out[it] = total(nv.at[it, 2], nz) / (point_total * moment_total)
        drain(n_z.at[it, pl.ds(0, nz - 1)], recv, it, N_Z)
        quads = total(n_z.at[it], nz)
        scale_s = 1.0 / jnp.sqrt(quads[:, :rank] / point_total + 1e-6)
        scale_u = 1.0 / jnp.sqrt(quads[:, rank:] / moment_total + 1e-6)

    s_out[...] = s_nx[ITERS - 1] * scale_s
    u_out[...] = u_nx[ITERS - 1] * scale_u
    for it in range(ITERS):
        for m in range(2):
            drain(cr.at[it, pl.ds(2 * m, 2)], send, it, m)
        small = nv.at[it, 0, pl.ds(0, 7)]
        for stage, ref in (
            (X_SUM, xr.at[it]), (Y_SUM, yr.at[it]), (Z_SUM, zr.at[it]), (Z_ALL, zr.at[it]),
            (C_ALL, cr.at[it]), (M_CX, small), (M_Y, small), (M_Z, small),
            (N_XY, n_xy.at[it, pl.ds(0, len(plane))]), (N_Z, n_z.at[it, pl.ds(0, nz - 1)]),
        ):
            drain(ref, send, it, stage)
        for d in NEAR:
            drain(yr.at[it, 0], send, it, Y_ALL + d)
        for d in range(NY):
            drain(xr.at[it, 0, pl.ds(0, (NX - 1) * yrows)], send, it, X_ALL + d)


def store(s, u, mis, s_out, u_out, mis_out, sem):
    copies = [pltpu.make_async_copy(u, u_out, sem.at[0]), pltpu.make_async_copy(s, s_out, sem.at[1])]
    for cp in copies:
        cp.start()
    for k in range(ITERS):
        mis_out[k] = jnp.sum(mis[k])
    for cp in copies:
        cp.wait()


def shards(nz, s0, u0, sig, rate, power, inv_s, inv_t):
    points, rank = s0.shape
    moments = u0.shape[0]
    half = moments // NC
    xrows = half // NX
    yrows = xrows // NY
    zrows = points // nz
    blocks = moments // xrows
    vmem, smem = pl.BlockSpec(memory_space=pltpu.VMEM), pl.BlockSpec(memory_space=pltpu.SMEM)
    hbm = pl.BlockSpec(memory_space=pltpu.HBM)
    outs = (
        jax.ShapeDtypeStruct((points, rank), F32),
        jax.ShapeDtypeStruct((moments, rank), F32),
        jax.ShapeDtypeStruct((ITERS,), F32),
    )
    modes = pl.pallas_call(
        functools.partial(kernel, nz),
        out_shape=outs[:2] + (jax.ShapeDtypeStruct((ITERS, 1, 128), F32),),
        in_specs=[hbm] * 7,
        out_specs=(vmem, vmem, vmem),
        scratch_shapes=[
            pltpu.VMEM((points, rank), F32),
            pltpu.VMEM((moments, rank), F32),
            pltpu.VMEM((blocks, points, xrows), F32),
            pltpu.VMEM((points // 128, 128), F32),
            pltpu.VMEM((points // 128, 128), F32),
            pltpu.VMEM((rank, rank), F32),
            pltpu.VMEM((rank, rank), F32),
            pltpu.VMEM((points, 128), F32),
            pltpu.VMEM((points, 128), F32),
            pltpu.VMEM((points, 128), F32),
            pltpu.VMEM((points, 128), F32),
            pltpu.VMEM((points, 2 * rank), BF16),
            pltpu.VMEM((2 * rank, points), BF16),
            pltpu.VMEM((moments, 4 * rank), BF16),
            pltpu.VMEM((2, points, 2 * xrows), F32),
            pltpu.VMEM((points, moments), BF16),
            pltpu.VMEM((points, moments), BF16),
            pltpu.VMEM((ITERS, NX, xrows, rank), F32),
            pltpu.VMEM((ITERS, NX, xrows, rank), F32),
            pltpu.VMEM((ITERS, NX, xrows, rank), F32),
            pltpu.VMEM((ITERS, NX - 1, xrows, rank), F32),
            pltpu.VMEM((ITERS, xrows, rank), F32),
            pltpu.VMEM((ITERS, NY - 1, yrows, rank), F32),
            pltpu.VMEM((ITERS, moments, rank), F32),
            pltpu.VMEM((ITERS, points, rank), F32),
            pltpu.VMEM((ITERS, nz - 1, zrows, rank), F32),
            pltpu.VMEM((ITERS, points, rank), F32),
            pltpu.VMEM((ITERS, 3, 8, 1, 128), F32),
            pltpu.VMEM((ITERS, NX * NY * NC, 1, 2 * rank), F32),
            pltpu.VMEM((ITERS, nz, 1, 2 * rank), F32),
            pltpu.SemaphoreType.DMA((6 + blocks,)),
            pltpu.SemaphoreType.DMA((ITERS, STAGES)),
            pltpu.SemaphoreType.DMA((ITERS, STAGES)),
        ],
        compiler_params=pltpu.CompilerParams(
            collective_id=0, has_side_effects=True, vmem_limit_bytes=40 * 1024 * 1024
        ),
    )(*[pltpu.with_memory_space_constraint(v, pltpu.HBM) for v in (
        s0, u0, sig, rate.reshape(points // 128, 128), power.reshape(points // 128, 128), inv_s, inv_t)])
    return pl.pallas_call(
        store,
        out_shape=outs,
        in_specs=[vmem, vmem, vmem],
        out_specs=(hbm, hbm, smem),
        scratch_shapes=[pltpu.SemaphoreType.DMA((2,))],
    )(*[pltpu.with_memory_space_constraint(v, pltpu.VMEM) for v in modes])


def solution(mesh):
    return jax.shard_map(
        functools.partial(shards, mesh.shape["tm"]),
        mesh=mesh,
        in_specs=(P("pts", None), P("tm", None), P("pts", "tm"), P("pts"), P("pts"), P(), P()),
        out_specs=(P("pts", None), P("tm", None), P()),
        check_vma=False,
    )
```

```python
import functools
import math

import jax
import jax.numpy as jnp
from jax import lax
from jax.experimental import pallas as pl
from jax.experimental.pallas import tpu as pltpu
from jax.sharding import PartitionSpec as P

ITERS = 2
F32, BF16 = jnp.float32, jnp.bfloat16
MESH = pl.DeviceIdType.MESH
NX, NY, NC = 4, 8, 2
ORDER = (2, 1, 3, 0)
NEAR = (1, 7, 2, 6, 3, 5, 4)
X_SUM, Y_SUM, Z_SUM, Z_ALL, C_ALL, N_XY, N_Z, M_CX, M_Y, M_Z, Y_ALL = range(2, 13)
X_ALL = Y_ALL + NY
STAGES = X_ALL + NY


def split(value):
    hi = value.astype(BF16)
    return hi, (value - hi.astype(F32)).astype(BF16)


def dot(a, b, ca, cb):
    return lax.dot_general(a, b, (((ca,), (cb,)), ((), ())), preferred_element_type=F32)


def kernel(nz, s_in, u_in, sig_in, rate_in, power_in, inv_s_in, inv_t_in, s_out, u_out, mis_out,
           s0, u0, sig, rate, power, inv_s, inv_t,
           sig_lr, sig_ex, lr, ex, a_ref, at_ref, b_ref, rec, fh, fl, tp, cr, th, xr, ts, yr, u_nx, sp, zr, s_nx, nv, n_xy, n_z,
           load, send, recv):
    points, rank = s0.shape
    moments = u0.shape[0]
    half = moments // NC
    xrows = half // NX
    yrows = xrows // NY
    zrows = points // nz
    blocks = moments // xrows
    point_total = points * NX * NY * NC
    moment_total = moments * nz
    p, z = lax.axis_index("pts"), lax.axis_index("tm")
    c, x, y = p % NC, (p // NC) % NX, p // (NC * NX)

    def at(cc, xx, yy):
        return (yy * NX + xx) * NC + cc

    cx_peers = []
    for dc in range(NC):
        for dx in range(NX):
            if dc or dx:
                cx_peers.append(((c + dc) % NC, (x + dx) % NX))
    y_peers = [(y + d) % NY for d in NEAR[::-1]]
    z_far = sorted(range(1, nz), key=lambda d: -min(d, nz - d))
    z_peers = [(z + d) % nz for d in z_far]
    turned = [pl.multiple_of(zz * zrows, zrows) for zz in z_peers + [z]]
    plane = []
    for dy in NEAR[::-1] + (0,):
        for dx in ORDER:
            for dc in (1, 0):
                if dc or dx or dy:
                    plane.append(at((c + dc) % NC, (x + dx) % NX, (y + dy) % NY))

    starts = []
    for side in (1 - c, c):
        for d in ORDER:
            starts.append(pl.multiple_of(side * half + (x + d) % NX * xrows, xrows))

    loads = []

    def fetch(src, dst):
        cp = pltpu.make_async_copy(src, dst, load.at[len(loads)])
        cp.start()
        loads.append(cp)
        return cp

    u_load, s_load = fetch(u_in, u0), fetch(s_in, s0)
    rate_load, power_load = fetch(rate_in, rate), fetch(power_in, power)
    def fetch_stress(slots):
        return [fetch(sig_in.at[:, pl.ds(starts[k], xrows)], sig.at[k]) for k in slots]

    sig_load = fetch_stress(range(2))

    barrier = pltpu.get_barrier_semaphore()
    for pp in plane:
        pl.semaphore_signal(barrier, inc=1, device_id=(pp, z), device_id_type=MESH)
    for zz in z_peers:
        pl.semaphore_signal(barrier, inc=1, device_id=(p, zz), device_id_type=MESH)

    def put(src, dst, it, stage, pp, zz):
        pltpu.make_async_remote_copy(
            src_ref=src, dst_ref=dst, send_sem=send.at[it, stage], recv_sem=recv.at[it, stage],
            device_id=(pp, zz), device_id_type=MESH,
        ).start()

    def drain(ref, sem, it, stage):
        pltpu.make_async_copy(ref, ref, sem.at[it, stage]).wait()

    def split_time(u_cur, slots):
        for k in slots:
            q = starts[k]
            rows = pl.ds(k * xrows, xrows)
            hi, lo = split(u_cur[pl.ds(q, xrows), :])
            b_ref[rows, :rank] = hi
            b_ref[rows, rank : 2 * rank] = hi
            b_ref[rows, 2 * rank : 3 * rank] = lo
            b_ref[rows, 3 * rank :] = lo

    def total(ref, count):
        sums = [ref[k] for k in range(4)]
        for k in range(4, count):
            sums[k % 4] = sums[k % 4] + ref[k]
        return (sums[0] + sums[1]) + (sums[2] + sums[3])

    rate_load.wait()
    power_load.wait()
    for k in range(points // 128):
        rows = pl.ds(k * 128, 128)
        sig_lr[rows, :] = jnp.broadcast_to(jnp.log2(rate[k : k + 1, :]), (128, 128)).T
        sig_ex[rows, :] = jnp.broadcast_to(0.5 * (power[k : k + 1, :] - 1.0), (128, 128)).T
    for r, q in enumerate(turned):
        rows = pl.ds(r * zrows, zrows)
        lr[rows, :] = sig_lr[pl.ds(q, zrows), :]
        ex[rows, :] = sig_ex[pl.ds(q, zrows), :]
    u_load.wait()
    sig_load += fetch_stress(range(2, blocks))
    inv_loads = [fetch(inv_s_in, inv_s), fetch(inv_t_in, inv_t)]
    split_time(u0, range(blocks))
    s_load.wait()

    scale_s = scale_u = None
    for it in range(ITERS):
        s_cur = s0 if it == 0 else s_nx.at[it - 1]
        root = 1.0 / math.sqrt(rank)
        factor = root if it == 0 else scale_s * scale_u * root
        def turned_modes(k):
            return jnp.concatenate([s_cur[pl.ds(q, zrows), :] for q in turned[2 * k : 2 * k + 2]], axis=0) * factor

        for k in range(nz // 2):
            rows = pl.ds(2 * k * zrows, 2 * zrows)
            hi, lo = split(turned_modes(k))
            a_ref[rows, :rank] = hi
            a_ref[rows, rank:] = lo

        def transpose_modes():
            for k in range(nz // 2):
                rows = pl.ds(2 * k * zrows, 2 * zrows)
                hi, lo = split(turned_modes(k).T)
                at_ref[:rank, rows] = hi
                at_ref[rank:, rows] = lo

        def rebuild(m):
            rows = pl.ds(2 * m * xrows, 2 * xrows)
            for pts in (pl.ds(0, points // 2), pl.ds(points // 2, points // 2)):
                rec[m % 2, pts, :] = dot(a_ref[pts, :], b_ref[rows, : 2 * rank], 1, 1) + dot(
                    a_ref[pts, :], b_ref[rows, 2 * rank :], 1, 1)

        def respond(m, mis):
            for k in (2 * m, 2 * m + 1):
                lanes = pl.ds(k * xrows, xrows)
                for r, q in enumerate(turned):
                    rows = pl.ds(r * zrows, zrows)
                    stress = sig[k, pl.ds(q, zrows), :] - rec[m % 2, rows, pl.ds((k % 2) * xrows, xrows)]
                    quad = stress * stress
                    mis = mis + jnp.sum(quad.reshape(zrows // 8, 8, 128), axis=0)
                    flow = stress * jnp.exp2(lr[rows, :] + ex[rows, :] * jnp.log2(quad + 1e-6))
                    hi, lo = split(flow)
                    fh[rows, lanes] = hi
                    fl[rows, lanes] = lo
            return mis

        def time_part(m):
            lanes = pl.ds(2 * m * xrows, 2 * xrows)
            pair = dot(at_ref[...], fh[:, lanes], 1, 0)
            part = pair[:rank] + pair[rank:] + dot(at_ref[:rank, :], fl[:, lanes], 1, 0)
            return part[:, :xrows].T, part[:, xrows:].T

        def send_space(h):
            pts = pl.ds(h * (points // 2), points // 2)
            pair = dot(fh[pts, :], b_ref[:, rank : 3 * rank], 1, 0)
            sp[it, pts, :] = pair[:, :rank] + pair[:, rank:] + dot(fl[pts, :], b_ref[:, :rank], 1, 0)
            for r in range(h * nz // 2, min((h + 1) * nz // 2, nz - 1)):
                put(sp.at[it, pl.ds(r * zrows, zrows), :], zr.at[it, r], it, Z_SUM, p, z_peers[r])

        def keep_core(m, parts):
            for j in range(2):
                tp[it, 2 * m + j] = parts[j]

        def send_core(m):
            two = pl.ds(2 * m, 2)
            put(tp.at[it, two], cr.at[it, two], it, m, at(1 - c, x, y), z)

        def send_x(m, parts):
            drain(cr.at[it, pl.ds(2 * m, 2)], recv, it, m)
            for j in (2 * m, 2 * m + 1):
                th[it, j] = parts[j % 2] + cr[it, j]
                d = ORDER[j]
                if d:
                    put(th.at[it, j], xr.at[it, d - 1], it, X_SUM, at(c, (x + d) % NX, y), z)

        def arrive(m):
            if it == 0:
                sig_load[2 * m].wait()
                sig_load[2 * m + 1].wait()

        mis = jnp.zeros((8, 128), F32)
        rebuild(0)
        arrive(0)
        rebuild(1)
        transpose_modes()
        mis = respond(0, mis)
        keep_core(0, time_part(0))
        if it > 0:
            send_core(0)
        arrive(1)
        rebuild(2)
        mis = respond(1, mis)
        keep_core(1, time_part(1))
        if it > 0:
            send_core(1)
        arrive(2)
        rebuild(3)
        mis = respond(2, mis)
        parts = time_part(2)
        if it > 0:
            send_x(0, parts)
        else:
            pl.semaphore_wait(barrier, len(plane) + len(z_peers))
            send_core(0)
            send_core(1)
        arrive(3)
        mis = respond(3, mis)
        if it == 0:
            send_x(0, parts)
        send_x(1, time_part(3))
        send_space(0)
        send_space(1)
        last = it + 1 == ITERS
        me = c * NX + x
        nv[0, me, :, it * 128 : (it + 1) * 128] = jnp.sum(mis, axis=0, keepdims=True)
        if last:
            for cc, xx in cx_peers:
                put(nv.at[0, me], nv.at[0, me], it, M_CX, at(cc, xx, y), z)

        drain(xr.at[it], recv, it, X_SUM)
        ts[it] = th[it, NX - 1] + xr[it, 0] + xr[it, 1] + xr[it, 2]
        for d, yy in enumerate(y_peers):
            rows = pl.ds(pl.multiple_of(yy * yrows, yrows), yrows)
            put(ts.at[it, rows, :], yr.at[it, d], it, Y_SUM, at(c, x, yy), z)
        if it == 0:
            for cp in inv_loads:
                cp.wait()
        if last:
            drain(nv.at[0, pl.ds(0, 7)], recv, it, M_CX)
            nv[1, y] = total(nv.at[0], NC * NX)
            for yy in y_peers:
                put(nv.at[1, y], nv.at[1, y], it, M_Y, at(c, x, yy), z)

        def piece_rows(xx, yy):
            return pl.ds(pl.multiple_of(c * half + xx * xrows + yy * yrows, yrows), yrows)

        def pass_x(dy):
            rows = piece_rows(x, (y + NY - dy) % NY)
            for d in ORDER[: NX - 1]:
                put(u_nx.at[it, rows, :], u_nx.at[it, rows, :], it, X_ALL + dy, at(c, (x + d) % NX, y), z)

        def pass_core(dy):
            drain(xr.at[it, 0, pl.ds(0, (NX - 1) * yrows)], recv, it, X_ALL + dy)
            for d in ORDER[: NX - 1]:
                rows = piece_rows((x + d) % NX, (y + NY - dy) % NY)
                put(u_nx.at[it, rows, :], u_nx.at[it, rows, :], it, C_ALL, at(1 - c, x, y), z)

        drain(zr.at[it], recv, it, Z_SUM)
        own_z = pl.ds(pl.multiple_of(z * zrows, zrows), zrows)
        piece = sp[it, pl.ds((nz - 1) * zrows, zrows), :]
        for d in range(nz - 1):
            piece = piece + zr[it, d]
        if it > 0:
            piece = piece * scale_u
        s_raw = jnp.dot(piece, inv_s[...], precision=lax.Precision.HIGHEST, preferred_element_type=F32)
        s_nx[it, own_z, :] = s_raw
        n_xy[it, p, :, :rank] = jnp.sum(s_raw * s_raw, axis=0, keepdims=True)
        for zz in z_peers:
            put(s_nx.at[it, own_z, :], s_nx.at[it, own_z, :], it, Z_ALL, p, zz)

        drain(yr.at[it], recv, it, Y_SUM)
        rows = pl.ds(pl.multiple_of(y * yrows, yrows), yrows)
        piece = ts[it, rows, :]
        for d in range(NY - 1):
            piece = piece + yr[it, d]
        piece = piece * (math.sqrt(rank) if it == 0 else math.sqrt(rank) / scale_u)
        t_raw = jnp.dot(piece, inv_t[...], precision=lax.Precision.HIGHEST, preferred_element_type=F32)
        own_t = piece_rows(x, y)
        u_nx[it, own_t, :] = t_raw
        n_xy[it, p, :, rank:] = jnp.sum(t_raw * t_raw, axis=0, keepdims=True)
        for pp in plane:
            put(n_xy.at[it, p], n_xy.at[it, p], it, N_XY, pp, z)
        for d in NEAR[::-1]:
            put(u_nx.at[it, own_t, :], u_nx.at[it, own_t, :], it, Y_ALL + d, at(c, x, (y + d) % NY), z)
        pass_x(0)

        if last:
            drain(nv.at[1, pl.ds(0, 7)], recv, it, M_Y)
            nv[2, z] = total(nv.at[1], NY)
            for zz in z_peers:
                put(nv.at[2, z], nv.at[2, z], it, M_Z, p, zz)

        for d in NEAR:
            drain(u_nx.at[it, piece_rows(x, (y + NY - d) % NY), :], recv, it, Y_ALL + d)
            pass_x(d)
        drain(n_xy.at[it, pl.ds(0, len(plane))], recv, it, N_XY)
        n_z[it, z] = total(n_xy.at[it], len(plane) + 1)
        for zz in z_peers:
            put(n_z.at[it, z], n_z.at[it, z], it, N_Z, p, zz)
        own = pl.ds(pl.multiple_of(c * half + x * xrows, xrows), xrows)
        put(u_nx.at[it, own, :], u_nx.at[it, own, :], it, C_ALL, at(1 - c, x, y), z)
        for d in (0,) + NEAR[:2]:
            pass_core(d)
        for d in NEAR[2:]:
            pass_core(d)
        if it + 1 < ITERS:
            split_time(u_nx.at[it], range(NX, 2 * NX))
        drain(cr.at[it], recv, it, C_ALL)
        if it + 1 < ITERS:
            split_time(u_nx.at[it], range(NX))
        drain(zr.at[it], recv, it, Z_ALL)
        if last:
            drain(nv.at[2, pl.ds(0, 7)], recv, it, M_Z)
            mis_out[...] = total(nv.at[2], nz) / (point_total * moment_total)
        drain(n_z.at[it, pl.ds(0, nz - 1)], recv, it, N_Z)
        quads = total(n_z.at[it], nz)
        scale_s = 1.0 / jnp.sqrt(quads[:, :rank] / point_total + 1e-6)
        scale_u = 1.0 / jnp.sqrt(quads[:, rank:] / moment_total + 1e-6)

    s_out[...] = s_nx[ITERS - 1] * scale_s
    u_out[...] = u_nx[ITERS - 1] * scale_u
    for it in range(ITERS):
        for m in range(2):
            drain(cr.at[it, pl.ds(2 * m, 2)], send, it, m)
        for stage, ref in (
            (X_SUM, xr.at[it]), (Y_SUM, yr.at[it]), (Z_SUM, zr.at[it]), (Z_ALL, zr.at[it]),
            (C_ALL, cr.at[it]),
            (N_XY, n_xy.at[it, pl.ds(0, len(plane))]), (N_Z, n_z.at[it, pl.ds(0, nz - 1)]),
        ):
            drain(ref, send, it, stage)
        if it + 1 == ITERS:
            for stage in (M_CX, M_Y, M_Z):
                drain(nv.at[0, pl.ds(0, 7)], send, it, stage)
        for d in NEAR:
            drain(yr.at[it, 0], send, it, Y_ALL + d)
        for d in range(NY):
            drain(xr.at[it, 0, pl.ds(0, (NX - 1) * yrows)], send, it, X_ALL + d)


def store(s, u, mis, s_out, u_out, mis_out, sem):
    copies = [pltpu.make_async_copy(u, u_out, sem.at[0]), pltpu.make_async_copy(s, s_out, sem.at[1])]
    for cp in copies:
        cp.start()
    for k in range(ITERS):
        mis_out[k] = jnp.sum(mis[:, k * 128 : (k + 1) * 128])
    for cp in copies:
        cp.wait()


def shards(nz, s0, u0, sig, rate, power, inv_s, inv_t):
    points, rank = s0.shape
    moments = u0.shape[0]
    half = moments // NC
    xrows = half // NX
    yrows = xrows // NY
    zrows = points // nz
    blocks = moments // xrows
    vmem, smem = pl.BlockSpec(memory_space=pltpu.VMEM), pl.BlockSpec(memory_space=pltpu.SMEM)
    hbm = pl.BlockSpec(memory_space=pltpu.HBM)
    outs = (
        jax.ShapeDtypeStruct((points, rank), F32),
        jax.ShapeDtypeStruct((moments, rank), F32),
        jax.ShapeDtypeStruct((ITERS,), F32),
    )
    modes = pl.pallas_call(
        functools.partial(kernel, nz),
        out_shape=outs[:2] + (jax.ShapeDtypeStruct((1, ITERS * 128), F32),),
        in_specs=[hbm] * 7,
        out_specs=(vmem, vmem, vmem),
        scratch_shapes=[
            pltpu.VMEM((points, rank), F32),
            pltpu.VMEM((moments, rank), F32),
            pltpu.VMEM((blocks, points, xrows), F32),
            pltpu.VMEM((points // 128, 128), F32),
            pltpu.VMEM((points // 128, 128), F32),
            pltpu.VMEM((rank, rank), F32),
            pltpu.VMEM((rank, rank), F32),
            pltpu.VMEM((points, 128), F32),
            pltpu.VMEM((points, 128), F32),
            pltpu.VMEM((points, 128), F32),
            pltpu.VMEM((points, 128), F32),
            pltpu.VMEM((points, 2 * rank), BF16),
            pltpu.VMEM((2 * rank, points), BF16),
            pltpu.VMEM((moments, 4 * rank), BF16),
            pltpu.VMEM((2, points, 2 * xrows), F32),
            pltpu.VMEM((points, moments), BF16),
            pltpu.VMEM((points, moments), BF16),
            pltpu.VMEM((ITERS, NX, xrows, rank), F32),
            pltpu.VMEM((ITERS, NX, xrows, rank), F32),
            pltpu.VMEM((ITERS, NX, xrows, rank), F32),
            pltpu.VMEM((ITERS, NX - 1, xrows, rank), F32),
            pltpu.VMEM((ITERS, xrows, rank), F32),
            pltpu.VMEM((ITERS, NY - 1, yrows, rank), F32),
            pltpu.VMEM((ITERS, moments, rank), F32),
            pltpu.VMEM((ITERS, points, rank), F32),
            pltpu.VMEM((ITERS, nz - 1, zrows, rank), F32),
            pltpu.VMEM((ITERS, points, rank), F32),
            pltpu.VMEM((3, 8, 1, ITERS * 128), F32),
            pltpu.VMEM((ITERS, NX * NY * NC, 1, 2 * rank), F32),
            pltpu.VMEM((ITERS, nz, 1, 2 * rank), F32),
            pltpu.SemaphoreType.DMA((6 + blocks,)),
            pltpu.SemaphoreType.DMA((ITERS, STAGES)),
            pltpu.SemaphoreType.DMA((ITERS, STAGES)),
        ],
        compiler_params=pltpu.CompilerParams(
            collective_id=0, has_side_effects=True, vmem_limit_bytes=40 * 1024 * 1024
        ),
    )(*[pltpu.with_memory_space_constraint(v, pltpu.HBM) for v in (
        s0, u0, sig, rate.reshape(points // 128, 128), power.reshape(points // 128, 128), inv_s, inv_t)])
    return pl.pallas_call(
        store,
        out_shape=outs,
        in_specs=[vmem, vmem, vmem],
        out_specs=(hbm, hbm, smem),
        scratch_shapes=[pltpu.SemaphoreType.DMA((2,))],
    )(*[pltpu.with_memory_space_constraint(v, pltpu.VMEM) for v in modes])


def solution(mesh):
    return jax.shard_map(
        functools.partial(shards, mesh.shape["tm"]),
        mesh=mesh,
        in_specs=(P("pts", None), P("tm", None), P("pts", "tm"), P("pts"), P("pts"), P(), P()),
        out_specs=(P("pts", None), P("tm", None), P()),
        check_vma=False,
    )
```

```python
import functools
import math

import jax
import jax.numpy as jnp
from jax import lax
from jax.experimental import pallas as pl
from jax.experimental.pallas import tpu as pltpu
from jax.sharding import PartitionSpec as P

ITERS = 2
F32, BF16 = jnp.float32, jnp.bfloat16
MESH = pl.DeviceIdType.MESH
NX, NY, NC = 4, 8, 2
ORDER = (2, 1, 3, 0)
NEAR = (1, 7, 2, 6, 3, 5, 4)
X_SUM, Y_SUM, Z_SUM, Z_ALL, C_ALL, N_XY, N_Z, M_CX, M_Y, M_Z, Y_ALL = range(2, 13)
X_ALL = Y_ALL + NY
STAGES = X_ALL + NY


def split(value):
    hi = value.astype(BF16)
    return hi, (value - hi.astype(F32)).astype(BF16)


def dot(a, b, ca, cb):
    return lax.dot_general(a, b, (((ca,), (cb,)), ((), ())), preferred_element_type=F32)


def kernel(nz, s_in, u_in, sig_in, rate_in, power_in, inv_s_in, inv_t_in, s_out, u_out, mis_out,
           s0, u0, sig, rate, power, inv_s, inv_t,
           raw_fluid, raw_expo, fluid, ex, a_ref, at_ref, b_ref, rec, fh, fl, tp, cr, th, xr, ts, yr, u_nx, sp, zr, s_nx, nv, n_xy, n_z,
           load, send, recv):
    points, rank = s0.shape
    moments = u0.shape[0]
    half = moments // NC
    xrows = half // NX
    yrows = xrows // NY
    zrows = points // nz
    blocks = moments // xrows
    point_total = points * NX * NY * NC
    moment_total = moments * nz
    p, z = lax.axis_index("pts"), lax.axis_index("tm")
    c, x, y = p % NC, (p // NC) % NX, p // (NC * NX)

    def at(cc, xx, yy):
        return (yy * NX + xx) * NC + cc

    cx_peers = []
    for dc in range(NC):
        for dx in range(NX):
            if dc or dx:
                cx_peers.append(((c + dc) % NC, (x + dx) % NX))
    y_peers = [(y + d) % NY for d in NEAR[::-1]]
    z_far = sorted(range(1, nz), key=lambda d: -min(d, nz - d))
    z_peers = [(z + d) % nz for d in z_far]
    turned = [pl.multiple_of(zz * zrows, zrows) for zz in z_peers + [z]]
    plane = []
    for dy in NEAR[::-1] + (0,):
        for dx in ORDER:
            for dc in (1, 0):
                if dc or dx or dy:
                    plane.append(at((c + dc) % NC, (x + dx) % NX, (y + dy) % NY))

    starts = []
    for side in (1 - c, c):
        for d in ORDER:
            starts.append(pl.multiple_of(side * half + (x + d) % NX * xrows, xrows))

    loads = []

    def fetch(src, dst):
        cp = pltpu.make_async_copy(src, dst, load.at[len(loads)])
        cp.start()
        loads.append(cp)
        return cp

    u_load, s_load = fetch(u_in, u0), fetch(s_in, s0)
    rate_load, power_load = fetch(rate_in, rate), fetch(power_in, power)
    def fetch_stress(slots):
        return [fetch(sig_in.at[:, pl.ds(starts[k], xrows)], sig.at[k]) for k in slots]

    sig_load = fetch_stress(range(2))

    barrier = pltpu.get_barrier_semaphore()
    for pp in plane:
        pl.semaphore_signal(barrier, inc=1, device_id=(pp, z), device_id_type=MESH)
    for zz in z_peers:
        pl.semaphore_signal(barrier, inc=1, device_id=(p, zz), device_id_type=MESH)

    def put(src, dst, it, stage, pp, zz):
        pltpu.make_async_remote_copy(
            src_ref=src, dst_ref=dst, send_sem=send.at[it, stage], recv_sem=recv.at[it, stage],
            device_id=(pp, zz), device_id_type=MESH,
        ).start()

    def drain(ref, sem, it, stage):
        pltpu.make_async_copy(ref, ref, sem.at[it, stage]).wait()

    def split_time(u_cur, slots):
        for k in slots:
            q = starts[k]
            rows = pl.ds(k * xrows, xrows)
            hi, lo = split(u_cur[pl.ds(q, xrows), :])
            b_ref[rows, :rank] = hi
            b_ref[rows, rank : 2 * rank] = hi
            b_ref[rows, 2 * rank : 3 * rank] = lo
            b_ref[rows, 3 * rank :] = lo

    def total(ref, count):
        sums = [ref[k] for k in range(4)]
        for k in range(4, count):
            sums[k % 4] = sums[k % 4] + ref[k]
        return (sums[0] + sums[1]) + (sums[2] + sums[3])

    rate_load.wait()
    power_load.wait()
    for k in range(points // 128):
        rows = pl.ds(k * 128, 128)
        raw_fluid[rows, :] = jnp.broadcast_to(rate[k : k + 1, :], (128, 128)).T
        raw_expo[rows, :] = jnp.broadcast_to(0.5 * (power[k : k + 1, :] - 1.0), (128, 128)).T
    for r, q in enumerate(turned):
        rows = pl.ds(r * zrows, zrows)
        fluid[rows, :] = raw_fluid[pl.ds(q, zrows), :]
        ex[rows, :] = raw_expo[pl.ds(q, zrows), :]
    u_load.wait()
    sig_load += fetch_stress(range(2, blocks))
    inv_loads = [fetch(inv_s_in, inv_s), fetch(inv_t_in, inv_t)]
    split_time(u0, range(blocks))
    s_load.wait()

    scale_s = scale_u = None
    for it in range(ITERS):
        s_cur = s0 if it == 0 else s_nx.at[it - 1]
        root = 1.0 / math.sqrt(rank)
        factor = root if it == 0 else scale_s * scale_u * root
        def turned_modes(k):
            return jnp.concatenate([s_cur[pl.ds(q, zrows), :] for q in turned[2 * k : 2 * k + 2]], axis=0) * factor

        for k in range(nz // 2):
            rows = pl.ds(2 * k * zrows, 2 * zrows)
            hi, lo = split(turned_modes(k))
            a_ref[rows, :rank] = hi
            a_ref[rows, rank:] = lo

        def transpose_modes():
            for k in range(nz // 2):
                rows = pl.ds(2 * k * zrows, 2 * zrows)
                hi, lo = split((turned_modes(k) * fluid[rows, :]).T)
                at_ref[:rank, rows] = hi
                at_ref[rank:, rows] = lo

        def rebuild(m):
            rows = pl.ds(2 * m * xrows, 2 * xrows)
            for pts in (pl.ds(0, points // 2), pl.ds(points // 2, points // 2)):
                rec[m % 2, pts, :] = dot(a_ref[pts, :], b_ref[rows, : 2 * rank], 1, 1) + dot(
                    a_ref[pts, :], b_ref[rows, 2 * rank :], 1, 1)

        def respond(m, mis):
            for k in (2 * m, 2 * m + 1):
                lanes = pl.ds(k * xrows, xrows)
                for r, q in enumerate(turned):
                    rows = pl.ds(r * zrows, zrows)
                    stress = sig[k, pl.ds(q, zrows), :] - rec[m % 2, rows, pl.ds((k % 2) * xrows, xrows)]
                    quad = stress * stress
                    mis = mis + jnp.sum(quad.reshape(zrows // 8, 8, 128), axis=0)
                    flow = stress * jnp.exp2(ex[rows, :] * jnp.log2(quad + 1e-6))
                    hi, lo = split(flow)
                    fh[rows, lanes] = hi
                    fl[rows, lanes] = lo
            return mis

        def time_part(m):
            lanes = pl.ds(2 * m * xrows, 2 * xrows)
            pair = dot(at_ref[...], fh[:, lanes], 1, 0)
            part = pair[:rank] + pair[rank:] + dot(at_ref[:rank, :], fl[:, lanes], 1, 0)
            return part[:, :xrows].T, part[:, xrows:].T

        def send_space(h):
            pts = pl.ds(h * (points // 2), points // 2)
            pair = dot(fh[pts, :], b_ref[:, rank : 3 * rank], 1, 0)
            sp[it, pts, :] = fluid[pts, :] * (pair[:, :rank] + pair[:, rank:] + dot(fl[pts, :], b_ref[:, :rank], 1, 0))
            for r in range(h * nz // 2, min((h + 1) * nz // 2, nz - 1)):
                put(sp.at[it, pl.ds(r * zrows, zrows), :], zr.at[it, r], it, Z_SUM, p, z_peers[r])

        def keep_core(m, parts):
            for j in range(2):
                tp[it, 2 * m + j] = parts[j]

        def send_core(m):
            two = pl.ds(2 * m, 2)
            put(tp.at[it, two], cr.at[it, two], it, m, at(1 - c, x, y), z)

        def send_x(m, parts):
            drain(cr.at[it, pl.ds(2 * m, 2)], recv, it, m)
            for j in (2 * m, 2 * m + 1):
                th[it, j] = parts[j % 2] + cr[it, j]
                d = ORDER[j]
                if d:
                    put(th.at[it, j], xr.at[it, d - 1], it, X_SUM, at(c, (x + d) % NX, y), z)

        def arrive(m):
            if it == 0:
                sig_load[2 * m].wait()
                sig_load[2 * m + 1].wait()

        mis = jnp.zeros((8, 128), F32)
        rebuild(0)
        arrive(0)
        rebuild(1)
        transpose_modes()
        mis = respond(0, mis)
        keep_core(0, time_part(0))
        if it > 0:
            send_core(0)
        arrive(1)
        rebuild(2)
        mis = respond(1, mis)
        keep_core(1, time_part(1))
        if it > 0:
            send_core(1)
        arrive(2)
        rebuild(3)
        mis = respond(2, mis)
        parts = time_part(2)
        if it > 0:
            send_x(0, parts)
        else:
            pl.semaphore_wait(barrier, len(plane) + len(z_peers))
            send_core(0)
            send_core(1)
        arrive(3)
        mis = respond(3, mis)
        if it == 0:
            send_x(0, parts)
        send_x(1, time_part(3))
        send_space(0)
        send_space(1)
        last = it + 1 == ITERS
        me = c * NX + x
        nv[0, me, :, it * 128 : (it + 1) * 128] = jnp.sum(mis, axis=0, keepdims=True)
        if last:
            for cc, xx in cx_peers:
                put(nv.at[0, me], nv.at[0, me], it, M_CX, at(cc, xx, y), z)

        drain(xr.at[it], recv, it, X_SUM)
        ts[it] = th[it, NX - 1] + xr[it, 0] + xr[it, 1] + xr[it, 2]
        for d, yy in enumerate(y_peers):
            rows = pl.ds(pl.multiple_of(yy * yrows, yrows), yrows)
            put(ts.at[it, rows, :], yr.at[it, d], it, Y_SUM, at(c, x, yy), z)
        if it == 0:
            for cp in inv_loads:
                cp.wait()
        if last:
            drain(nv.at[0, pl.ds(0, 7)], recv, it, M_CX)
            nv[1, y] = total(nv.at[0], NC * NX)
            for yy in y_peers:
                put(nv.at[1, y], nv.at[1, y], it, M_Y, at(c, x, yy), z)

        def piece_rows(xx, yy):
            return pl.ds(pl.multiple_of(c * half + xx * xrows + yy * yrows, yrows), yrows)

        def pass_x(dy):
            rows = piece_rows(x, (y + NY - dy) % NY)
            for d in ORDER[: NX - 1]:
                put(u_nx.at[it, rows, :], u_nx.at[it, rows, :], it, X_ALL + dy, at(c, (x + d) % NX, y), z)

        def pass_core(dy):
            drain(xr.at[it, 0, pl.ds(0, (NX - 1) * yrows)], recv, it, X_ALL + dy)
            for d in ORDER[: NX - 1]:
                rows = piece_rows((x + d) % NX, (y + NY - dy) % NY)
                put(u_nx.at[it, rows, :], u_nx.at[it, rows, :], it, C_ALL, at(1 - c, x, y), z)

        drain(zr.at[it], recv, it, Z_SUM)
        own_z = pl.ds(pl.multiple_of(z * zrows, zrows), zrows)
        piece = sp[it, pl.ds((nz - 1) * zrows, zrows), :]
        for d in range(nz - 1):
            piece = piece + zr[it, d]
        if it > 0:
            piece = piece * scale_u
        s_raw = jnp.dot(piece, inv_s[...], precision=lax.Precision.HIGHEST, preferred_element_type=F32)
        s_nx[it, own_z, :] = s_raw
        n_xy[it, p, :, :rank] = jnp.sum(s_raw * s_raw, axis=0, keepdims=True)
        for zz in z_peers:
            put(s_nx.at[it, own_z, :], s_nx.at[it, own_z, :], it, Z_ALL, p, zz)

        drain(yr.at[it], recv, it, Y_SUM)
        rows = pl.ds(pl.multiple_of(y * yrows, yrows), yrows)
        piece = ts[it, rows, :]
        for d in range(NY - 1):
            piece = piece + yr[it, d]
        piece = piece * (math.sqrt(rank) if it == 0 else math.sqrt(rank) / scale_u)
        t_raw = jnp.dot(piece, inv_t[...], precision=lax.Precision.HIGHEST, preferred_element_type=F32)
        own_t = piece_rows(x, y)
        u_nx[it, own_t, :] = t_raw
        n_xy[it, p, :, rank:] = jnp.sum(t_raw * t_raw, axis=0, keepdims=True)
        for pp in plane:
            put(n_xy.at[it, p], n_xy.at[it, p], it, N_XY, pp, z)
        for d in NEAR[::-1]:
            put(u_nx.at[it, own_t, :], u_nx.at[it, own_t, :], it, Y_ALL + d, at(c, x, (y + d) % NY), z)
        pass_x(0)

        if last:
            drain(nv.at[1, pl.ds(0, 7)], recv, it, M_Y)
            nv[2, z] = total(nv.at[1], NY)
            for zz in z_peers:
                put(nv.at[2, z], nv.at[2, z], it, M_Z, p, zz)

        for d in NEAR:
            drain(u_nx.at[it, piece_rows(x, (y + NY - d) % NY), :], recv, it, Y_ALL + d)
            pass_x(d)
        drain(n_xy.at[it, pl.ds(0, len(plane))], recv, it, N_XY)
        n_z[it, z] = total(n_xy.at[it], len(plane) + 1)
        for zz in z_peers:
            put(n_z.at[it, z], n_z.at[it, z], it, N_Z, p, zz)
        own = pl.ds(pl.multiple_of(c * half + x * xrows, xrows), xrows)
        put(u_nx.at[it, own, :], u_nx.at[it, own, :], it, C_ALL, at(1 - c, x, y), z)
        for d in (0,) + NEAR[:2]:
            pass_core(d)
        for d in NEAR[2:]:
            pass_core(d)
        if it + 1 < ITERS:
            split_time(u_nx.at[it], range(NX, 2 * NX))
        drain(cr.at[it], recv, it, C_ALL)
        if it + 1 < ITERS:
            split_time(u_nx.at[it], range(NX))
        drain(zr.at[it], recv, it, Z_ALL)
        if last:
            drain(nv.at[2, pl.ds(0, 7)], recv, it, M_Z)
            mis_out[...] = total(nv.at[2], nz) / (point_total * moment_total)
        drain(n_z.at[it, pl.ds(0, nz - 1)], recv, it, N_Z)
        quads = total(n_z.at[it], nz)
        scale_s = 1.0 / jnp.sqrt(quads[:, :rank] / point_total + 1e-6)
        scale_u = 1.0 / jnp.sqrt(quads[:, rank:] / moment_total + 1e-6)

    s_out[...] = s_nx[ITERS - 1] * scale_s
    u_out[...] = u_nx[ITERS - 1] * scale_u
    for it in range(ITERS):
        for m in range(2):
            drain(cr.at[it, pl.ds(2 * m, 2)], send, it, m)
        for stage, ref in (
            (X_SUM, xr.at[it]), (Y_SUM, yr.at[it]), (Z_SUM, zr.at[it]), (Z_ALL, zr.at[it]),
            (C_ALL, cr.at[it]),
            (N_XY, n_xy.at[it, pl.ds(0, len(plane))]), (N_Z, n_z.at[it, pl.ds(0, nz - 1)]),
        ):
            drain(ref, send, it, stage)
        if it + 1 == ITERS:
            for stage in (M_CX, M_Y, M_Z):
                drain(nv.at[0, pl.ds(0, 7)], send, it, stage)
        for d in NEAR:
            drain(yr.at[it, 0], send, it, Y_ALL + d)
        for d in range(NY):
            drain(xr.at[it, 0, pl.ds(0, (NX - 1) * yrows)], send, it, X_ALL + d)


def store(s, u, mis, s_out, u_out, mis_out, sem):
    copies = [pltpu.make_async_copy(u, u_out, sem.at[0]), pltpu.make_async_copy(s, s_out, sem.at[1])]
    for cp in copies:
        cp.start()
    for k in range(ITERS):
        mis_out[k] = jnp.sum(mis[:, k * 128 : (k + 1) * 128])
    for cp in copies:
        cp.wait()


def shards(nz, s0, u0, sig, rate, power, inv_s, inv_t):
    points, rank = s0.shape
    moments = u0.shape[0]
    half = moments // NC
    xrows = half // NX
    yrows = xrows // NY
    zrows = points // nz
    blocks = moments // xrows
    vmem, smem = pl.BlockSpec(memory_space=pltpu.VMEM), pl.BlockSpec(memory_space=pltpu.SMEM)
    hbm = pl.BlockSpec(memory_space=pltpu.HBM)
    outs = (
        jax.ShapeDtypeStruct((points, rank), F32),
        jax.ShapeDtypeStruct((moments, rank), F32),
        jax.ShapeDtypeStruct((ITERS,), F32),
    )
    modes = pl.pallas_call(
        functools.partial(kernel, nz),
        out_shape=outs[:2] + (jax.ShapeDtypeStruct((1, ITERS * 128), F32),),
        in_specs=[hbm] * 7,
        out_specs=(vmem, vmem, vmem),
        scratch_shapes=[
            pltpu.VMEM((points, rank), F32),
            pltpu.VMEM((moments, rank), F32),
            pltpu.VMEM((blocks, points, xrows), F32),
            pltpu.VMEM((points // 128, 128), F32),
            pltpu.VMEM((points // 128, 128), F32),
            pltpu.VMEM((rank, rank), F32),
            pltpu.VMEM((rank, rank), F32),
            pltpu.VMEM((points, 128), F32),
            pltpu.VMEM((points, 128), F32),
            pltpu.VMEM((points, 128), F32),
            pltpu.VMEM((points, 128), F32),
            pltpu.VMEM((points, 2 * rank), BF16),
            pltpu.VMEM((2 * rank, points), BF16),
            pltpu.VMEM((moments, 4 * rank), BF16),
            pltpu.VMEM((2, points, 2 * xrows), F32),
            pltpu.VMEM((points, moments), BF16),
            pltpu.VMEM((points, moments), BF16),
            pltpu.VMEM((ITERS, NX, xrows, rank), F32),
            pltpu.VMEM((ITERS, NX, xrows, rank), F32),
            pltpu.VMEM((ITERS, NX, xrows, rank), F32),
            pltpu.VMEM((ITERS, NX - 1, xrows, rank), F32),
            pltpu.VMEM((ITERS, xrows, rank), F32),
            pltpu.VMEM((ITERS, NY - 1, yrows, rank), F32),
            pltpu.VMEM((ITERS, moments, rank), F32),
            pltpu.VMEM((ITERS, points, rank), F32),
            pltpu.VMEM((ITERS, nz - 1, zrows, rank), F32),
            pltpu.VMEM((ITERS, points, rank), F32),
            pltpu.VMEM((3, 8, 1, ITERS * 128), F32),
            pltpu.VMEM((ITERS, NX * NY * NC, 1, 2 * rank), F32),
            pltpu.VMEM((ITERS, nz, 1, 2 * rank), F32),
            pltpu.SemaphoreType.DMA((6 + blocks,)),
            pltpu.SemaphoreType.DMA((ITERS, STAGES)),
            pltpu.SemaphoreType.DMA((ITERS, STAGES)),
        ],
        compiler_params=pltpu.CompilerParams(
            collective_id=0, has_side_effects=True, vmem_limit_bytes=40 * 1024 * 1024
        ),
    )(*[pltpu.with_memory_space_constraint(v, pltpu.HBM) for v in (
        s0, u0, sig, rate.reshape(points // 128, 128), power.reshape(points // 128, 128), inv_s, inv_t)])
    return pl.pallas_call(
        store,
        out_shape=outs,
        in_specs=[vmem, vmem, vmem],
        out_specs=(hbm, hbm, smem),
        scratch_shapes=[pltpu.SemaphoreType.DMA((2,))],
    )(*[pltpu.with_memory_space_constraint(v, pltpu.VMEM) for v in modes])


def solution(mesh):
    return jax.shard_map(
        functools.partial(shards, mesh.shape["tm"]),
        mesh=mesh,
        in_specs=(P("pts", None), P("tm", None), P("pts", "tm"), P("pts"), P("pts"), P(), P()),
        out_specs=(P("pts", None), P("tm", None), P()),
        check_vma=False,
    )
```
